32 devices in a mesh: seq: 8 (over y, x, core), fsdp: 4 (over z).
Axes of the slice: x: 2, y: 2, z: 4, core: 2. Of those that a mesh axis runs over, the one named last changes fastest.
Arguments:
- block_input: float32 [4, 1024, 1024], P('fsdp', 'seq'), may hold values from -6 to 6
- attn_gain: bfloat16 [1024], P('fsdp'), may hold values from 0.099609375 to 1.8984375
- query_weight: bfloat16 [1024, 512], P('fsdp'), may hold values from -0.1875 to 0.1875
- key_weight: bfloat16 [1024, 512], P('fsdp'), may hold values from -0.1875 to 0.1875
- value_weight: bfloat16 [1024, 1024], P('fsdp'), may hold values from -0.1875 to 0.1875
- gate_weight: bfloat16 [1024, 1024], P('fsdp'), may hold values from -0.1875 to 0.1875
- decay_down: bfloat16 [1024, 16], P('fsdp'), may hold values from -0.1875 to 0.1875
- decay_up: bfloat16 [16, 512], P(None, 'fsdp'), may hold values from -1.5 to 1.5
- decay_bias: bfloat16 [512], P('fsdp'), may hold values from -0.5 to 11
- head_gain: bfloat16 [256], P('fsdp'), may hold values from 0.099609375 to 1.8984375
- out_weight: bfloat16 [1024, 1024], P('fsdp'), may hold values from -0.375 to 0.375
- ffn_gain: bfloat16 [1024], P('fsdp'), may hold values from 0.099609375 to 1.8984375
- ffn_gate: bfloat16 [1024, 2816], P('fsdp'), may hold values from -0.1875 to 0.1875
- ffn_up: bfloat16 [1024, 2816], P('fsdp'), may hold values from -0.1875 to 0.1875
- ffn_down: bfloat16 [2816, 1024], P(None, 'fsdp'), may hold values from -0.21875 to 0.21875
- cotangent: float32 [4, 1024, 1024], P('fsdp', 'seq'), may hold values from -6 to 6
Outputs:
- block_output: float32 [4, 1024, 1024], P('fsdp', 'seq')
- input_grad: float32 [4, 1024, 1024], P('fsdp', 'seq')
- grad_attn_gain: float32 [1024], P(('seq', 'fsdp'))
- grad_query: float32 [1024, 512], P(('seq', 'fsdp'))
- grad_key: float32 [1024, 512], P(('seq', 'fsdp'))
- grad_value: float32 [1024, 1024], P(('seq', 'fsdp'))
- grad_gate: float32 [1024, 1024], P(('seq', 'fsdp'))
- grad_decay_down: float32 [1024, 16], P(('seq', 'fsdp'))
- grad_decay_up: float32 [16, 512], P(None, ('seq', 'fsdp'))
- grad_decay_bias: float32 [512], P(('seq', 'fsdp'))
- grad_head_gain: float32 [256], P(('seq', 'fsdp'))
- grad_out: float32 [1024, 1024], P(('seq', 'fsdp'))
- grad_ffn_gain: float32 [1024], P(('seq', 'fsdp'))
- grad_ffn_gate: float32 [1024, 2816], P(('seq', 'fsdp'))
- grad_ffn_up: float32 [1024, 2816], P(('seq', 'fsdp'))
- grad_ffn_down: float32 [2816, 1024], P(None, ('seq', 'fsdp'))
The draws below stay inside these ranges and needn't reach their ends.
All inputs are finite; a program needn't handle non-finite values.
Results may differ from the reference program's by a relative error of at most 0.039.
Values may be sent and summed in bfloat16 or wider, within the bound.
A program may use at most 192 MiB of HBM per device.

```python
import jax
import jax.numpy as jnp
from jax import lax

D = 1024
H = 4
HK = 128
HV = 256
R = 16
FF = 2816
BLOCK = 64
KD = 512
VD = 1024
SEQS = 4
LEN = 1024


def draw_decay_bias(key, part):
    pick_key, slow_key, fast_key, place_key = jax.random.split(jax.random.fold_in(key, 17), 4)
    keep_share = 0.5
    slow_mask = jax.random.bernoulli(pick_key, keep_share, (KD,))
    log_length = jnp.log(jnp.float32(LEN))
    slow_value = log_length + jax.random.uniform(slow_key, (KD,), jnp.float32, -2.5, 0.5)
    fast_value = jax.random.uniform(fast_key, (KD,), jnp.float32, -0.5, 1.5)
    values = jnp.where(slow_mask, slow_value, fast_value)
    order = jax.random.permutation(place_key, KD)
    values = values.at[order[0]].set(11.0)
    values = values.at[order[1]].set(-0.5)
    return values.astype(jnp.bfloat16)


def strengthened(array, stream_key, source, target, shards_of, factor):
    def block_of(axis_at):
        return (jnp.arange(array.shape[axis_at]) // (array.shape[axis_at] // shards_of)).reshape((-1,) + (1,) * (array.ndim - 1 - axis_at))

    one_side = jax.random.permutation(stream_key, shards_of)[block_of(target)]
    far = (block_of(target) + shards_of // 2) % shards_of
    return jnp.where((block_of(source) == one_side) | (block_of(source) == far), factor * array, array)


def level_of(stream_key, shape, cuts, smallest, top_value):
    factor_of, own = 1.0, jax.random.fold_in(stream_key, 6)
    for axis_at, parts in cuts:
        draws = jnp.exp(jax.random.uniform(jax.random.fold_in(own, axis_at), (parts,), jnp.float32, smallest / len(cuts), top_value / len(cuts)))
        factor_of = factor_of * jnp.repeat(draws, shape[axis_at] // parts).reshape([-1 if axis == axis_at else 1 for axis in range(len(shape))])
    return factor_of


def gaussian(key, dims, deviation, most, cuts=(), held_as=jnp.bfloat16):
    loudness = level_of(key, dims, cuts, -0.22, 0.18) if cuts else 1.0
    drawn = jax.random.normal(key, dims, jnp.float32) * deviation * loudness
    return jnp.minimum(jnp.maximum(drawn, -most), most).astype(held_as)


def noise_with(key, shape, width, bound, cuts, heavy, kind=jnp.bfloat16):
    values = width * jax.random.normal(key, shape, jnp.float32)
    if cuts:
        values = values * level_of(key, shape, cuts, -0.22, 0.18)
    return jnp.clip(strengthened(values, jax.random.fold_in(key, 3), *heavy), -bound, bound).astype(kind)


def setup_inputs(seed: int = 0) -> dict:
    key_of = jax.random.split(jax.random.key(seed), 17)
    return {
        "block_input": gaussian(key_of[0], (SEQS, LEN, D), 1.0, 6.0, ((0, 4), (1, 8)), jnp.float32),
        "attn_gain": jnp.clip(1.0 + 0.18 * jax.random.normal(key_of[1], (D,), jnp.float32), 0.099609375, 1.8984375).astype(jnp.bfloat16),
        "query_weight": gaussian(key_of[2], (D, KD), D ** -0.5, 0.1875, ((0, 4),)),
        "key_weight": gaussian(key_of[3], (D, KD), D ** -0.5, 0.1875, ((0, 4),)),
        "value_weight": gaussian(key_of[4], (D, VD), D ** -0.5, 0.1875, ((0, 4),)),
        "gate_weight": gaussian(key_of[5], (D, VD), D ** -0.5, 0.1875, ((0, 4),)),
        "decay_down": gaussian(key_of[6], (D, R), D ** -0.5, 0.1875, ((0, 4),)),
        "decay_up": gaussian(key_of[7], (R, KD), R ** -0.5, 1.5, ((1, 4),)),
        "decay_bias": draw_decay_bias(jax.random.fold_in(key_of[16], 71), 0),
        "head_gain": jnp.clip(1.0 + 0.18 * jax.random.normal(key_of[9], (HV,), jnp.float32), 0.099609375, 1.8984375).astype(jnp.bfloat16),
        "out_weight": gaussian(key_of[10], (VD, D), (VD // 4) ** -0.5, 0.375, ((0, 4),)),
        "ffn_gain": jnp.clip(1.0 + 0.18 * jax.random.normal(key_of[11], (D,), jnp.float32), 0.099609375, 1.8984375).astype(jnp.bfloat16),
        "ffn_gate": gaussian(key_of[12], (D, FF), D ** -0.5, 0.1875, ((0, 4),)),
        "ffn_up": gaussian(key_of[13], (D, FF), D ** -0.5, 0.1875, ((0, 4),)),
        "ffn_down": gaussian(key_of[14], (FF, D), (FF // 4) ** -0.5, 0.21875, ((1, 4),)),
        "cotangent": noise_with(key_of[15], (SEQS, LEN, D), 1.0, 6.0, ((0, 4), (1, 8)), (1, 2, 8, 2.0), jnp.float32),
    }


norm_eps = 1e-06
logit_norm = 16.0
highest_precision = lax.Precision.HIGHEST

def product(left, right):
    return jnp.dot(left, right, preferred_element_type=jnp.float32)

def transposed(left, right):
    return jnp.dot(left.T, right, preferred_element_type=jnp.float32)

def rms_gain(token_rows, gain_row):
    return token_rows * lax.rsqrt(lax.optimization_barrier(jnp.mean(token_rows * token_rows, axis=-1, keepdims=True)) + norm_eps) * gain_row

def gated_norm(attended, gate_pre, head_gain):
    head_rows = attended.reshape(attended.shape[0], H, HV)
    gate_acts = jax.nn.silu(gate_pre.reshape(head_rows.shape))
    return (rms_gain(head_rows, head_gain) * gate_acts).reshape(attended.shape[0], H * HV)

def swiglu(gate_part, up_part):
    return jax.nn.silu(gate_part) * up_part

def block_scan(queries, key_rows, value_rows, log_decay):
    length = queries.shape[0]
    blocks = length // BLOCK
    key_scaling_factor = HK ** (-0.5)
    lower_mask = jnp.arange(BLOCK)[:, None] >= jnp.arange(BLOCK)[None, :]

    def advance(carried_state, pieces):
        query_part, key_part, value_portion, decay_part = pieces
        running = jnp.cumsum(decay_part, axis=0)
        block_count_total = running[-1]
        query_decayed = query_part * jnp.exp(running)
        key_dec = key_part * jnp.exp(-running)
        key_final_decay = key_part * jnp.exp(block_count_total[None] - running)
        scores = jnp.einsum('thk,shk->hts', query_decayed, key_dec, precision=highest_precision)
        scores = jnp.where(lower_mask[None], scores, 0.0)
        output_rows = jnp.einsum('hts,shv->thv', scores, value_portion, precision=highest_precision)
        output_rows = output_rows + jnp.einsum('qse,seg->qsg', query_decayed, carried_state, precision=highest_precision)
        carried_state = jnp.exp(block_count_total)[:, :, None] * carried_state + jnp.einsum('ufn,ufm->fnm', key_final_decay, value_portion, precision=highest_precision)
        return (carried_state, output_rows * key_scaling_factor)
    pieces = (queries.reshape(blocks, BLOCK, H, HK), key_rows.reshape(blocks, BLOCK, H, HK), value_rows.reshape(blocks, BLOCK, H, HV), log_decay.reshape(blocks, BLOCK, H, HK))
    zero_state = jnp.zeros((H, HK, HV), queries.dtype)
    carried_state, output_rows = lax.scan(advance, zero_state, pieces)
    return (output_rows.reshape(length, H * HV), carried_state)

def sequence_pass(token_rows, cot_rows, attn_params, ffn_params):
    attn_gain, query_weight, key_weight, value_weight, gate_weight, decay_down, decay_up, decay_bias, head_gain, out_weight = attn_params
    ffn_gain, ffn_gate, ffn_up, ffn_down = ffn_params
    normed_one, norm_one_back = jax.vjp(rms_gain, token_rows, attn_gain.astype(jnp.float32))
    hidden_one = normed_one.astype(jnp.bfloat16)
    queries = product(hidden_one, query_weight).astype(jnp.bfloat16)
    key_rows = product(hidden_one, key_weight).astype(jnp.bfloat16)
    value_rows = product(hidden_one, value_weight).astype(jnp.bfloat16)
    gate_pre = product(hidden_one, gate_weight)
    low_rank = product(hidden_one, decay_down).astype(jnp.bfloat16)
    logits = product(low_rank, decay_up) + decay_bias.astype(jnp.float32)
    log_decay = jax.nn.log_sigmoid(logits) / logit_norm
    attended, scan_back, final_state = jax.vjp(block_scan, queries.astype(jnp.float32), key_rows.astype(jnp.float32), value_rows.astype(jnp.float32), log_decay, has_aux=True)
    gated, gated_back = jax.vjp(gated_norm, attended, gate_pre, head_gain.astype(jnp.float32))
    gated_low = gated.astype(jnp.bfloat16)
    residual = token_rows + product(gated_low, out_weight)
    normed_two, norm_two_back = jax.vjp(rms_gain, residual, ffn_gain.astype(jnp.float32))
    hidden_two = normed_two.astype(jnp.bfloat16)
    ffn_gate_pre = product(hidden_two, ffn_gate)
    ffn_up_pre = product(hidden_two, ffn_up)
    mixed, mixed_back = jax.vjp(swiglu, ffn_gate_pre, ffn_up_pre)
    mixed_low = mixed.astype(jnp.bfloat16)
    block_output = residual + product(mixed_low, ffn_down)
    cot_low = cot_rows.astype(jnp.bfloat16)
    grad_ffn_down = transposed(mixed_low, cot_low)
    d_gate_part, d_up_part = mixed_back(product(cot_low, ffn_down.T))
    d_gate_low = d_gate_part.astype(jnp.bfloat16)
    d_up_low = d_up_part.astype(jnp.bfloat16)
    grad_ffn_gate = transposed(hidden_two, d_gate_low)
    grad_ffn_up = transposed(hidden_two, d_up_low)
    d_hidden_two = product(d_gate_low, ffn_gate.T) + product(d_up_low, ffn_up.T)
    d_residual_norm, grad_ffn_gain = norm_two_back(d_hidden_two)
    d_residual = cot_rows + d_residual_norm
    d_res_low = d_residual.astype(jnp.bfloat16)
    grad_out = transposed(gated_low, d_res_low)
    d_attended, d_gate_pre, grad_head_gain = gated_back(product(d_res_low, out_weight.T))
    d_queries, d_keys, d_values, d_log_decay = scan_back(d_attended)
    d_logits = d_log_decay * jax.nn.sigmoid(-logits) / logit_norm
    grad_decay_bias = lax.optimization_barrier(jnp.sum(d_logits, axis=0))
    d_logits_low = d_logits.astype(jnp.bfloat16)
    grad_decay_up = transposed(low_rank, d_logits_low)
    d_low_rank = product(d_logits_low, decay_up.T).astype(jnp.bfloat16)
    grad_decay_down = transposed(hidden_one, d_low_rank)
    d_query_low = d_queries.astype(jnp.bfloat16)
    d_key_low = d_keys.astype(jnp.bfloat16)
    d_value_low = d_values.astype(jnp.bfloat16)
    d_gate_one = d_gate_pre.astype(jnp.bfloat16)
    grad_query = transposed(hidden_one, d_query_low)
    grad_key = transposed(hidden_one, d_key_low)
    grad_value = transposed(hidden_one, d_value_low)
    grad_gate = transposed(hidden_one, d_gate_one)
    d_hidden_one = product(d_query_low, query_weight.T) + product(d_key_low, key_weight.T) + product(d_value_low, value_weight.T) + product(d_gate_one, gate_weight.T) + product(d_low_rank, decay_down.T)
    d_input_norm, grad_attn_gain = norm_one_back(d_hidden_one)
    input_grad = d_residual + d_input_norm
    attn_grads = (grad_attn_gain, grad_query, grad_key, grad_value, grad_gate, grad_decay_down, grad_decay_up, grad_decay_bias, grad_head_gain, grad_out)
    ffn_grads = (grad_ffn_gain, grad_ffn_gate, grad_ffn_up, grad_ffn_down)
    return (block_output, input_grad, attn_grads, ffn_grads)

def reference(block_input, attn_gain, query_weight, key_weight, value_weight, gate_weight, decay_down, decay_up, decay_bias, head_gain, out_weight, ffn_gain, ffn_gate, ffn_up, ffn_down, cotangent):
    attn_params = (attn_gain, query_weight, key_weight, value_weight, gate_weight, decay_down, decay_up, decay_bias, head_gain, out_weight)
    ffn_params = (ffn_gain, ffn_gate, ffn_up, ffn_down)
    output_list = []
    input_list = []
    attn_total = None
    ffn_total = None
    for seq_index in range(SEQS):
        block_output, input_grad, attn_grads, ffn_grads = sequence_pass(block_input[seq_index], cotangent[seq_index], attn_params, ffn_params)
        output_list.append(block_output)
        input_list.append(input_grad)
        if attn_total is None:
            attn_total = attn_grads
            ffn_total = ffn_grads
        else:
            attn_total = jax.tree.map(jnp.add, attn_total, attn_grads)
            ffn_total = jax.tree.map(jnp.add, ffn_total, ffn_grads)
    grad_attn_gain, grad_query, grad_key, grad_value, grad_gate, grad_decay_down, grad_decay_up, grad_decay_bias, grad_head_gain, grad_out = attn_total
    grad_ffn_gain, grad_ffn_gate, grad_ffn_up, grad_ffn_down = ffn_total
    return (jnp.stack(output_list), jnp.stack(input_list), grad_attn_gain, grad_query, grad_key, grad_value, grad_gate, grad_decay_down, grad_decay_up, grad_decay_bias, grad_head_gain, grad_out, grad_ffn_gain, grad_ffn_gate, grad_ffn_up, grad_ffn_down)
```

```python
import jax
import jax.numpy as jnp
from jax import lax
from jax.sharding import PartitionSpec as P

HK = 128
HV = 256
BLOCK = 64


norm_eps = 1e-06
logit_norm = 16.0
exact = lax.Precision.HIGHEST
fine = lax.Precision.HIGH
low = jnp.bfloat16
wide = jnp.float32


def product(left, right):
    return jnp.dot(left, right, preferred_element_type=wide)


def transposed(left, right):
    return lax.dot_general(left, right, (((0,), (0,)), ((), ())), preferred_element_type=wide)


def against(left, right):
    return lax.dot_general(left, right, (((1,), (1,)), ((), ())), preferred_element_type=wide)


def fine_dot(spec, left, right):
    return jnp.einsum(spec, left, right, precision=fine, preferred_element_type=wide)


def rms_gain(token_rows, gain_row):
    return (
        token_rows
        * lax.rsqrt(jnp.mean(token_rows * token_rows, axis=-1, keepdims=True) + norm_eps)
        * gain_row
    )


def gated_norm(attended, gate_pre, head_gain):
    return rms_gain(attended, head_gain) * jax.nn.silu(gate_pre)


def swiglu(gate_part, up_part):
    return jax.nn.silu(gate_part) * up_part


def exchange(pieces):
    return lax.all_to_all(pieces, "fsdp", 0, 0)


def gather_rows(rows):
    return lax.all_gather(rows, "fsdp", axis=0, tiled=True)


def scatter_rows(rows):
    return lax.psum_scatter(rows.astype(low), "fsdp", scatter_dimension=0, tiled=True).astype(wide)


def column_owned(weights, parts, si, shards):
    rows = weights[0].shape[0] // shards
    cuts = [
        lax.dynamic_slice_in_dim(w, si * rows, rows, 0).reshape(rows, parts, -1) for w in weights
    ]
    sent = jnp.concatenate(cuts, axis=2).transpose(1, 0, 2)
    got = lax.all_gather(exchange(sent), "seq")
    return got.transpose(1, 0, 2, 3).reshape(parts * shards * rows, -1)


def owned_columns(grads, parts):
    section = lax.psum_scatter(grads.astype(low), "seq", scatter_dimension=0, tiled=True)
    rows = section.shape[0] // parts
    return exchange(section.reshape(parts, rows, -1))


def across(pieces):
    rows = pieces.shape[1]
    return pieces.transpose(1, 0, 2).reshape(rows, -1).astype(wide)


def on_device(
    block_input,
    attn_gain,
    query_weight,
    key_weight,
    value_weight,
    gate_weight,
    decay_down,
    decay_up,
    decay_bias,
    head_gain,
    out_weight,
    ffn_gain,
    ffn_gate,
    ffn_up,
    ffn_down,
    cotangent,
):
    shards, parts = lax.axis_size("seq"), lax.axis_size("fsdp")
    si = lax.axis_index("seq")
    x = block_input[0]
    cot_rows = cotangent[0]
    length, width = x.shape
    blocks = length // BLOCK
    scale = HK ** (-0.5)

    small = lax.all_gather(
        jnp.concatenate([attn_gain, ffn_gain, head_gain, decay_down.reshape(-1)]), "fsdp"
    )
    own = attn_gain.shape[0]
    own_head = head_gain.shape[0]
    gain_one = small[:, :own].reshape(-1).astype(wide)
    gain_two = small[:, own : 2 * own].reshape(-1).astype(wide)
    gain_head = small[:, 2 * own : 2 * own + own_head].reshape(-1).astype(wide)
    down_full = small[:, 2 * own + own_head :].reshape(width, -1)
    rank = down_full.shape[1]

    normed_one, norm_one_back = jax.vjp(rms_gain, x, gain_one)
    hidden_one = gather_rows(normed_one.astype(low))
    attn_w = column_owned(
        (query_weight, key_weight, value_weight, gate_weight), parts, si, shards
    )
    cot_low = gather_rows(cot_rows.astype(low))
    ffn_w = column_owned((ffn_gate, ffn_up), parts, si, shards)
    ff = ffn_w.shape[1] // 2
    down_rows = ff // shards
    down_cut = lax.dynamic_slice_in_dim(
        ffn_down.reshape(parts, ff, own), si * down_rows, down_rows, 1
    )
    down_w = (
        lax.all_gather(exchange(down_cut), "seq").transpose(0, 2, 1, 3).reshape(ff, width)
    )

    projected = product(hidden_one, attn_w)
    rounded = projected[:, : 2 * HK + HV].astype(low)
    gate_pre = projected[:, 2 * HK + HV :]
    low_rank = product(hidden_one, down_full).astype(low)
    logits = product(low_rank, decay_up) + decay_bias.astype(wide)
    log_decay = jax.nn.log_sigmoid(logits) / logit_norm

    def chunked(rows):
        return rows.reshape(parts * blocks, BLOCK, -1)

    q = chunked(rounded[:, :HK].astype(wide))
    k = chunked(rounded[:, HK : 2 * HK].astype(wide))
    v = chunked(rounded[:, 2 * HK :].astype(wide))
    place = jnp.arange(BLOCK)
    lower = place[:, None] >= place[None, :]
    ones_lower = lower.astype(wide)
    running = jnp.einsum("ts,bsk->btk", ones_lower, chunked(log_decay), precision=exact)
    total = running[:, -1]
    grown = jnp.exp(running)
    shrunk = jnp.exp(-running)
    to_end = jnp.exp(total[:, None] - running)
    qd = q * grown
    kd = k * shrunk
    kf = k * to_end
    scores = jnp.where(lower[None], fine_dot("btk,bsk->bts", qd, kd), 0.0)
    intra = fine_dot("bts,bsv->btv", scores, v)
    added = fine_dot("bsk,bsv->bkv", kf, v)
    added_c = added.reshape(parts, blocks, HK, HV)
    total_c = total.reshape(parts, blocks, HK)
    factor_c = jnp.exp(total_c)[..., None]
    local_state = added_c[:, 0]
    for c in range(1, blocks):
        local_state = factor_c[:, c] * local_state + added_c[:, c]
    totals = lax.all_gather(jnp.sum(total_c, axis=1), "seq")
    states = lax.all_gather(local_state.astype(low), "seq")
    index = jnp.arange(shards)
    upto = jnp.cumsum(totals, axis=0)
    mine_upto = lax.dynamic_index_in_dim(upto, si, 0, False)
    mine_total = lax.dynamic_index_in_dim(totals, si, 0, False)
    before = (index < si)[:, None, None]
    after = (index > si)[:, None, None]
    early = jnp.where(before, jnp.exp(jnp.where(before, mine_upto - mine_total - upto, 0.0)), 0.0)
    late = jnp.where(
        after, jnp.exp(jnp.where(after, upto - totals - mine_upto, 0.0)), 0.0
    )
    incoming = jnp.sum(early[..., None] * states.astype(wide), axis=0)
    entering = [incoming]
    for c in range(blocks):
        entering.append(factor_c[:, c] * entering[-1] + added_c[:, c])
    state_in = jnp.stack(entering[:-1], axis=1).reshape(parts * blocks, HK, HV)
    state_out = jnp.stack(entering[1:], axis=1).reshape(parts * blocks, HK, HV)
    attended = scale * (intra + fine_dot("btk,bkv->btv", qd, state_in))
    attended = attended.reshape(parts * length, HV)

    gated, gated_back = jax.vjp(gated_norm, attended, gate_pre, gain_head)
    gated_low = gated.astype(low)
    residual = x + scatter_rows(product(gated_low, out_weight))
    normed_two, norm_two_back = jax.vjp(rms_gain, residual, gain_two)
    hidden_two = gather_rows(normed_two.astype(low))
    pre = product(hidden_two, ffn_w)
    mixed, mixed_back = jax.vjp(swiglu, pre[:, :ff], pre[:, ff:])
    mixed_low = mixed.astype(low)
    d_gate_part, d_up_part = mixed_back(against(cot_low, down_w))
    d_pre = jnp.concatenate([d_gate_part.astype(low), d_up_part.astype(low)], axis=1)
    d_residual_norm, grad_ffn_gain = norm_two_back(scatter_rows(against(d_pre, ffn_w)))
    d_residual = cot_rows + d_residual_norm
    d_res_low = gather_rows(d_residual.astype(low))
    block_output = residual + scatter_rows(product(mixed_low, down_w))
    ffn_owned = owned_columns(
        jnp.concatenate(
            [transposed(hidden_two, d_pre).astype(low), transposed(cot_low, mixed_low).astype(low)],
            axis=1,
        ),
        parts,
    )

    d_attended, d_gate_pre, grad_head_gain = gated_back(against(d_res_low, out_weight))
    d_out = chunked(scale * d_attended)
    pulled = fine_dot("btk,btv->bkv", qd, d_out)
    pulled_c = pulled.reshape(parts, blocks, HK, HV)
    local_pull = pulled_c[:, blocks - 1]
    for c in range(blocks - 2, -1, -1):
        local_pull = factor_c[:, c] * local_pull + pulled_c[:, c]
    pulls = lax.all_gather(local_pull.astype(low), "seq")
    later = jnp.sum(late[..., None] * pulls.astype(wide), axis=0)
    leaving = [later]
    for c in range(blocks - 1, 0, -1):
        leaving.insert(0, factor_c[:, c] * leaving[0] + pulled_c[:, c])
    d_state = jnp.stack(leaving, axis=1).reshape(parts * blocks, HK, HV)
    d_scores = jnp.where(lower[None], fine_dot("btv,bsv->bts", d_out, v), 0.0)
    d_q = grown * (
        fine_dot("bts,bsk->btk", d_scores, kd) + fine_dot("btv,bkv->btk", d_out, state_in)
    )
    d_k = shrunk * fine_dot("bts,btk->bsk", d_scores, qd) + to_end * fine_dot(
        "bsv,bkv->bsk", v, d_state
    )
    d_v = fine_dot("bts,btv->bsv", scores, d_out) + fine_dot("bsk,bkv->bsv", kf, d_state)
    tail_term = jnp.sum(d_state * state_out, axis=2)
    d_log_decay = (
        jnp.einsum("st,bsk->btk", ones_lower, q * d_q - k * d_k, precision=exact)
        + tail_term[:, None]
    )
    d_logits = d_log_decay.reshape(parts * length, HK) * jax.nn.sigmoid(-logits) / logit_norm
    grad_decay_bias = jnp.sum(d_logits, axis=0)
    d_logits_low = d_logits.astype(low)
    grad_decay_up = transposed(low_rank, d_logits_low)
    d_low_rank = against(d_logits_low, decay_up).astype(low)
    grad_decay_down = transposed(hidden_one, d_low_rank)
    d_projected = jnp.concatenate(
        [
            d_q.reshape(parts * length, HK).astype(low),
            d_k.reshape(parts * length, HK).astype(low),
            d_v.reshape(parts * length, HV).astype(low),
            d_gate_pre.astype(low),
        ],
        axis=1,
    )
    d_hidden_one = scatter_rows(against(d_projected, attn_w) + against(d_low_rank, down_full))
    d_input_norm, grad_attn_gain = norm_one_back(d_hidden_one)
    input_grad = d_residual + d_input_norm
    attn_owned = owned_columns(transposed(hidden_one, d_projected), parts)

    devices = shards * parts
    turned = [(s * parts + f, f * shards + s) for s in range(shards) for f in range(parts)]
    out_part = lax.psum_scatter(
        transposed(gated_low, d_res_low).astype(low), "seq", scatter_dimension=0, tiled=True
    )
    own_out = lax.ppermute(out_part, ("seq", "fsdp"), turned).astype(wide)
    head_part = lax.psum_scatter(
        jnp.concatenate(
            [
                grad_decay_up.reshape(rank, shards, -1).transpose(1, 0, 2).reshape(shards, -1),
                grad_decay_bias.reshape(shards, -1),
            ],
            axis=1,
        ),
        "seq",
        scatter_dimension=0,
        tiled=True,
    )
    head_part = lax.ppermute(head_part, ("seq", "fsdp"), turned)[0]
    own_bias_size = HK // shards
    own_up = head_part[: rank * own_bias_size].reshape(rank, own_bias_size)
    own_bias = head_part[rank * own_bias_size :]
    summed = jnp.concatenate(
        [
            grad_attn_gain.reshape(devices, -1),
            grad_ffn_gain.reshape(devices, -1),
            grad_head_gain.reshape(devices, -1),
            grad_decay_down.reshape(devices, -1),
        ],
        axis=1,
    )
    summed = lax.psum_scatter(summed, "seq", scatter_dimension=0, tiled=True)
    summed = lax.psum_scatter(summed, "fsdp", scatter_dimension=0, tiled=True)[0]
    each = width // devices
    each_head = HV // devices
    own_attn_gain = summed[:each]
    own_ffn_gain = summed[each : 2 * each]
    own_head_gain = summed[2 * each : 2 * each + each_head]
    own_down = summed[2 * each + each_head :].reshape(each, rank)
    return (
        block_output[None],
        input_grad[None],
        own_attn_gain,
        across(attn_owned[:, :, :HK]),
        across(attn_owned[:, :, HK : 2 * HK]),
        across(attn_owned[:, :, 2 * HK : 2 * HK + HV]),
        across(attn_owned[:, :, 2 * HK + HV :]),
        own_down,
        own_up,
        own_bias,
        own_head_gain,
        own_out,
        own_ffn_gain,
        across(ffn_owned[:, :, :ff]),
        across(ffn_owned[:, :, ff : 2 * ff]),
        across(ffn_owned[:, :, 2 * ff :]).T,
    )


def solution(mesh):
    return jax.shard_map(
        on_device,
        mesh=mesh,
        in_specs=(
            P("fsdp", "seq", None),
            P("fsdp"),
            P("fsdp", None),
            P("fsdp", None),
            P("fsdp", None),
            P("fsdp", None),
            P("fsdp", None),
            P(None, "fsdp"),
            P("fsdp"),
            P("fsdp"),
            P("fsdp", None),
            P("fsdp"),
            P("fsdp", None),
            P("fsdp", None),
            P(None, "fsdp"),
            P("fsdp", "seq", None),
        ),
        out_specs=(
            P("fsdp", "seq", None),
            P("fsdp", "seq", None),
            P(("seq", "fsdp")),
            P(("seq", "fsdp"), None),
            P(("seq", "fsdp"), None),
            P(("seq", "fsdp"), None),
            P(("seq", "fsdp"), None),
            P(("seq", "fsdp"), None),
            P(None, ("seq", "fsdp")),
            P(("seq", "fsdp")),
            P(("seq", "fsdp")),
            P(("seq", "fsdp"), None),
            P(("seq", "fsdp")),
            P(("seq", "fsdp"), None),
            P(("seq", "fsdp"), None),
            P(None, ("seq", "fsdp")),
        ),
        check_vma=False,
    )
```

```python
import jax
import jax.numpy as jnp
from jax import lax
from jax.sharding import PartitionSpec as P

HK = 128
HV = 256
BLOCK = 64


norm_eps = 1e-06
logit_norm = 16.0
exact = lax.Precision.HIGHEST
fine = lax.Precision.HIGH
low = jnp.bfloat16
wide = jnp.float32


def product(left, right):
    return jnp.dot(left, right, preferred_element_type=wide)


def transposed(left, right):
    return lax.dot_general(left, right, (((0,), (0,)), ((), ())), preferred_element_type=wide)


def against(left, right):
    return lax.dot_general(left, right, (((1,), (1,)), ((), ())), preferred_element_type=wide)


def fine_dot(spec, left, right):
    return jnp.einsum(spec, left, right, precision=fine, preferred_element_type=wide)


def rms_gain(token_rows, gain_row):
    return (
        token_rows
        * lax.rsqrt(jnp.mean(token_rows * token_rows, axis=-1, keepdims=True) + norm_eps)
        * gain_row
    )


def gated_norm(attended, gate_pre, head_gain):
    return rms_gain(attended, head_gain) * jax.nn.silu(gate_pre)


def swiglu(gate_part, up_part):
    return jax.nn.silu(gate_part) * up_part


def exchange(pieces):
    return lax.all_to_all(pieces, "fsdp", 0, 0)


def gather_rows(rows):
    return lax.all_gather(rows, "fsdp", axis=0, tiled=True)


def scatter_rows(rows):
    return lax.psum_scatter(rows.astype(low), "fsdp", scatter_dimension=0, tiled=True).astype(wide)


def summed_rows(grads):
    return lax.psum_scatter(grads.astype(low), "seq", scatter_dimension=0, tiled=True)


def owned_columns(section, parts):
    return exchange(section.reshape(parts, section.shape[0] // parts, -1))


def across(pieces):
    rows = pieces.shape[1]
    return pieces.transpose(1, 0, 2).reshape(rows, -1).astype(wide)


def on_device(
    block_input,
    attn_gain,
    query_weight,
    key_weight,
    value_weight,
    gate_weight,
    decay_down,
    decay_up,
    decay_bias,
    head_gain,
    out_weight,
    ffn_gain,
    ffn_gate,
    ffn_up,
    ffn_down,
    cotangent,
):
    shards, parts = lax.axis_size("seq"), lax.axis_size("fsdp")
    si = lax.axis_index("seq")
    x = block_input[0]
    cot_rows = cotangent[0]
    length, width = x.shape
    blocks = length // BLOCK
    scale = HK ** (-0.5)

    small = jnp.concatenate([attn_gain, ffn_gain, head_gain, decay_down.reshape(-1)])
    small = exchange(jnp.broadcast_to(small[None], (parts, small.shape[0])))
    own = attn_gain.shape[0]
    own_head = head_gain.shape[0]
    gain_one = small[:, :own].reshape(-1).astype(wide)
    gain_two = small[:, own : 2 * own].reshape(-1).astype(wide)
    gain_head = small[:, 2 * own : 2 * own + own_head].reshape(-1).astype(wide)
    down_full = small[:, 2 * own + own_head :].reshape(width, -1)
    rank = down_full.shape[1]

    normed_one, norm_one_back = jax.vjp(rms_gain, x, gain_one)
    both = gather_rows(jnp.concatenate([normed_one.astype(low), cot_rows.astype(low)], axis=1))
    hidden_one = both[:, :width]
    cot_low = both[:, width:]
    ff = ffn_gate.shape[1] // parts
    rows = own // shards
    down_rows = ff // shards
    cuts = [
        lax.dynamic_slice_in_dim(w, si * rows, rows, 0).reshape(rows, parts, -1).transpose(1, 0, 2)
        for w in (query_weight, key_weight, value_weight, gate_weight, ffn_gate, ffn_up)
    ]
    cuts.append(
        lax.dynamic_slice_in_dim(
            ffn_down.reshape(parts, ff, own), si * down_rows, down_rows, 1
        ).reshape(parts, rows, -1)
    )
    got = lax.all_gather(exchange(jnp.concatenate(cuts, axis=2)), "seq")
    attn_columns = 2 * HK + 2 * HV
    attn_w = got[..., :attn_columns].transpose(1, 0, 2, 3).reshape(width, -1)
    ffn_w = (
        got[..., attn_columns : attn_columns + 2 * ff].transpose(1, 0, 2, 3).reshape(width, -1)
    )
    down_w = (
        got[..., attn_columns + 2 * ff :]
        .reshape(shards, parts, down_rows, own)
        .transpose(0, 2, 1, 3)
        .reshape(ff, width)
    )

    projected = product(hidden_one, attn_w)
    rounded = projected[:, : 2 * HK + HV].astype(low)
    gate_pre = projected[:, 2 * HK + HV :]
    low_rank = product(hidden_one, down_full).astype(low)
    logits = product(low_rank, decay_up) + decay_bias.astype(wide)
    log_decay = jax.nn.log_sigmoid(logits) / logit_norm

    def chunked(rows):
        return rows.reshape(parts * blocks, BLOCK, -1)

    q = chunked(rounded[:, :HK].astype(wide))
    k = chunked(rounded[:, HK : 2 * HK].astype(wide))
    v = chunked(rounded[:, 2 * HK :].astype(wide))
    place = jnp.arange(BLOCK)
    lower = place[:, None] >= place[None, :]
    ones_lower = lower.astype(wide)
    running = jnp.einsum("ts,bsk->btk", ones_lower, chunked(log_decay), precision=exact)
    total = running[:, -1]
    grown = jnp.exp(running)
    shrunk = jnp.exp(-running)
    to_end = jnp.exp(total[:, None] - running)
    qd = q * grown
    kd = k * shrunk
    kf = k * to_end
    scores = jnp.where(lower[None], fine_dot("btk,bsk->bts", qd, kd), 0.0)
    intra = fine_dot("bts,bsv->btv", scores, v)
    added = fine_dot("bsk,bsv->bkv", kf, v)
    added_c = added.reshape(parts, blocks, HK, HV)
    total_c = total.reshape(parts, blocks, HK)
    factor_c = jnp.exp(total_c)[..., None]
    local_state = added_c[:, 0]
    for c in range(1, blocks):
        local_state = factor_c[:, c] * local_state + added_c[:, c]
    totals = lax.all_gather(jnp.sum(total_c, axis=1), "seq")
    states = lax.all_gather(local_state.astype(low), "seq")
    index = jnp.arange(shards)
    upto = jnp.cumsum(totals, axis=0)
    mine_upto = lax.dynamic_index_in_dim(upto, si, 0, False)
    mine_total = lax.dynamic_index_in_dim(totals, si, 0, False)
    before = (index < si)[:, None, None]
    after = (index > si)[:, None, None]
    early = jnp.where(before, jnp.exp(jnp.where(before, mine_upto - mine_total - upto, 0.0)), 0.0)
    late = jnp.where(
        after, jnp.exp(jnp.where(after, upto - totals - mine_upto, 0.0)), 0.0
    )
    incoming = jnp.sum(early[..., None] * states.astype(wide), axis=0)
    entering = [incoming]
    for c in range(blocks):
        entering.append(factor_c[:, c] * entering[-1] + added_c[:, c])
    state_in = jnp.stack(entering[:-1], axis=1).reshape(parts * blocks, HK, HV)
    state_out = jnp.stack(entering[1:], axis=1).reshape(parts * blocks, HK, HV)
    attended = scale * (intra + fine_dot("btk,bkv->btv", qd, state_in))
    attended = attended.reshape(parts * length, HV)

    gated, gated_back = jax.vjp(gated_norm, attended, gate_pre, gain_head)
    gated_low = gated.astype(low)
    residual = x + scatter_rows(product(gated_low, out_weight))
    normed_two, norm_two_back = jax.vjp(rms_gain, residual, gain_two)
    hidden_two = gather_rows(normed_two.astype(low))
    pre = product(hidden_two, ffn_w)
    mixed, mixed_back = jax.vjp(swiglu, pre[:, :ff], pre[:, ff:])
    mixed_low = mixed.astype(low)
    d_gate_part, d_up_part = mixed_back(against(cot_low, down_w))
    d_pre = jnp.concatenate([d_gate_part.astype(low), d_up_part.astype(low)], axis=1)
    both = scatter_rows(
        jnp.concatenate(
            [against(d_pre, ffn_w).astype(low), product(mixed_low, down_w).astype(low)], axis=1
        )
    )
    d_residual_norm, grad_ffn_gain = norm_two_back(both[:, :width])
    d_residual = cot_rows + d_residual_norm
    d_res_low = gather_rows(d_residual.astype(low))
    block_output = residual + both[:, width:]
    ffn_section = summed_rows(
        jnp.concatenate(
            [transposed(hidden_two, d_pre).astype(low), transposed(cot_low, mixed_low).astype(low)],
            axis=1,
        )
    )
    ffn_owned = owned_columns(ffn_section, parts)

    d_attended, d_gate_pre, grad_head_gain = gated_back(against(d_res_low, out_weight))
    d_out = chunked(scale * d_attended)
    pulled = fine_dot("btk,btv->bkv", qd, d_out)
    pulled_c = pulled.reshape(parts, blocks, HK, HV)
    local_pull = pulled_c[:, blocks - 1]
    for c in range(blocks - 2, -1, -1):
        local_pull = factor_c[:, c] * local_pull + pulled_c[:, c]
    pulls = lax.all_gather(local_pull.astype(low), "seq")
    later = jnp.sum(late[..., None] * pulls.astype(wide), axis=0)
    leaving = [later]
    for c in range(blocks - 1, 0, -1):
        leaving.insert(0, factor_c[:, c] * leaving[0] + pulled_c[:, c])
    d_state = jnp.stack(leaving, axis=1).reshape(parts * blocks, HK, HV)
    d_scores = jnp.where(lower[None], fine_dot("btv,bsv->bts", d_out, v), 0.0)
    d_q = grown * (
        fine_dot("bts,bsk->btk", d_scores, kd) + fine_dot("btv,bkv->btk", d_out, state_in)
    )
    d_k = shrunk * fine_dot("bts,btk->bsk", d_scores, qd) + to_end * fine_dot(
        "bsv,bkv->bsk", v, d_state
    )
    d_v = fine_dot("bts,btv->bsv", scores, d_out) + fine_dot("bsk,bkv->bsv", kf, d_state)
    tail_term = jnp.sum(d_state * state_out, axis=2)
    d_log_decay = (
        jnp.einsum("st,bsk->btk", ones_lower, q * d_q - k * d_k, precision=exact)
        + tail_term[:, None]
    )
    d_logits = d_log_decay.reshape(parts * length, HK) * jax.nn.sigmoid(-logits) / logit_norm
    grad_decay_bias = jnp.sum(d_logits, axis=0)
    d_logits_low = d_logits.astype(low)
    grad_decay_up = transposed(low_rank, d_logits_low)
    d_low_rank = against(d_logits_low, decay_up).astype(low)
    grad_decay_down = transposed(hidden_one, d_low_rank)
    d_projected = jnp.concatenate(
        [
            d_q.reshape(parts * length, HK).astype(low),
            d_k.reshape(parts * length, HK).astype(low),
            d_v.reshape(parts * length, HV).astype(low),
            d_gate_pre.astype(low),
        ],
        axis=1,
    )
    d_hidden_one = scatter_rows(against(d_projected, attn_w) + against(d_low_rank, down_full))
    d_input_norm, grad_attn_gain = norm_one_back(d_hidden_one)
    input_grad = d_residual + d_input_norm
    devices = shards * parts
    grad_out = transposed(gated_low, d_res_low).astype(low)
    attn_section = summed_rows(
        jnp.concatenate(
            [transposed(hidden_one, d_projected).astype(low), grad_out.reshape(width, HV)], axis=1
        )
    )
    attn_owned = owned_columns(attn_section[:, :attn_columns], parts)
    turned = [(s * parts + f, f * shards + s) for s in range(shards) for f in range(parts)]
    own_out = lax.ppermute(
        attn_section[:, attn_columns:].reshape(-1, width), ("seq", "fsdp"), turned
    ).astype(wide)
    head_part = jnp.concatenate(
        [
            grad_decay_up.reshape(rank, shards, -1).transpose(1, 0, 2).reshape(shards, -1),
            grad_decay_bias.reshape(shards, -1),
        ],
        axis=1,
    )
    mine = jnp.arange(parts)[:, None, None] == lax.axis_index("fsdp")
    head_part = jnp.where(mine, head_part[None], 0.0).reshape(devices, -1)
    own_bias_size = HK // shards
    summed = jnp.concatenate(
        [
            grad_attn_gain.reshape(devices, -1),
            grad_ffn_gain.reshape(devices, -1),
            grad_head_gain.reshape(devices, -1),
            grad_decay_down.reshape(devices, -1),
            head_part,
        ],
        axis=1,
    )
    summed = jnp.sum(lax.all_to_all(summed, ("seq", "fsdp"), 0, 0), axis=0)
    each = width // devices
    each_head = HV // devices
    own_attn_gain = summed[:each]
    own_ffn_gain = summed[each : 2 * each]
    own_head_gain = summed[2 * each : 2 * each + each_head]
    at_up = 2 * each + each_head + each * rank
    at_bias = at_up + rank * own_bias_size
    own_down = summed[2 * each + each_head : at_up].reshape(each, rank)
    own_up = summed[at_up:at_bias].reshape(rank, own_bias_size)
    own_bias = summed[at_bias:]
    return (
        block_output[None],
        input_grad[None],
        own_attn_gain,
        across(attn_owned[:, :, :HK]),
        across(attn_owned[:, :, HK : 2 * HK]),
        across(attn_owned[:, :, 2 * HK : 2 * HK + HV]),
        across(attn_owned[:, :, 2 * HK + HV :]),
        own_down,
        own_up,
        own_bias,
        own_head_gain,
        own_out,
        own_ffn_gain,
        across(ffn_owned[:, :, :ff]),
        across(ffn_owned[:, :, ff : 2 * ff]),
        across(ffn_owned[:, :, 2 * ff :]).T,
    )


def solution(mesh):
    return jax.shard_map(
        on_device,
        mesh=mesh,
        in_specs=(
            P("fsdp", "seq", None),
            P("fsdp"),
            P("fsdp", None),
            P("fsdp", None),
            P("fsdp", None),
            P("fsdp", None),
            P("fsdp", None),
            P(None, "fsdp"),
            P("fsdp"),
            P("fsdp"),
            P("fsdp", None),
            P("fsdp"),
            P("fsdp", None),
            P("fsdp", None),
            P(None, "fsdp"),
            P("fsdp", "seq", None),
        ),
        out_specs=(
            P("fsdp", "seq", None),
            P("fsdp", "seq", None),
            P(("seq", "fsdp")),
            P(("seq", "fsdp"), None),
            P(("seq", "fsdp"), None),
            P(("seq", "fsdp"), None),
            P(("seq", "fsdp"), None),
            P(("seq", "fsdp"), None),
            P(None, ("seq", "fsdp")),
            P(("seq", "fsdp")),
            P(("seq", "fsdp")),
            P(("seq", "fsdp"), None),
            P(("seq", "fsdp")),
            P(("seq", "fsdp"), None),
            P(("seq", "fsdp"), None),
            P(None, ("seq", "fsdp")),
        ),
        check_vma=False,
    )
```
